256 devices in a mesh: node: 64 (over x_hi, z, y), col: 4 (over x_lo, core).
Axes of the slice: x: 4 (x_hi: 2, x_lo: 2; x = x_hi * 2 + x_lo), y: 4, z: 8, core: 2. Of those that a mesh axis runs over, the one named last changes fastest.
Arguments:
- panel: bfloat16 [311296, 256], P('node', 'col'), may hold values from -6 to 6
- basis: bfloat16 [311296, 2048], P('node', 'col'), may hold values from -0.03125 to 0.03125
- g_blocks: bfloat16 [2432, 3, 128, 128], P('node'), may hold values from -0.3125 to 0.3125
- c_blocks: bfloat16 [2432, 3, 128, 128], P('node'), may hold values from -0.3125 to 0.3125
- block_cols: int32 [2432, 3], P('node'), may hold values from 0 to 2431, as said below
Outputs:
- reduced_g: float32 [2048, 256], P(('col', 'node'))
- reduced_c: float32 [2048, 256], P(('col', 'node'))
The draws below stay inside these ranges and needn't reach their ends.
Inputs may be any that keep to these rules, and one draw needn't show every extreme that they name: `block_cols`: block row i names block columns within 4 of i: the first is i itself, and one lies exactly 4 away wherever that stays inside the grid.
All inputs are finite; a program needn't handle non-finite values.
Results may differ from the reference program's by a relative error of at most 0.0029.
Values may be sent and summed in bfloat16 or wider, within the bound.
A program may use at most 64 MiB of HBM per device.

```python
import jax
import jax.numpy as jnp
from jax import lax

BS = 128
SLOTS = 3
HB = 4
K = 256
Q = 2048
NB = 2432
N = 311296


def draw_block_cols(key, part):
    first_key, second_key = jax.random.split(jax.random.fold_in(key, 17))
    row_ids = jnp.arange(NB, dtype=jnp.int32)
    nearby = jax.random.randint(first_key, (NB,), -HB, HB + 1).astype(jnp.int32)
    sides = (jax.random.randint(second_key, (NB,), 0, 2) * 2 - 1).astype(jnp.int32)
    stacked = jnp.stack([row_ids, row_ids + nearby, row_ids + sides * HB], 1)
    return jnp.clip(stacked, 0, NB - 1).astype(jnp.int32)


def raised(drawn, key, source, target, blocks, factor):
    def block_of(dim):
        return (jnp.arange(drawn.shape[dim]) // (drawn.shape[dim] // blocks)).reshape((-1,) + (1,) * (drawn.ndim - 1 - dim))

    first = jax.random.permutation(key, blocks)[block_of(target)]
    second = (block_of(target) + blocks // 2) % blocks
    return jnp.where((block_of(source) == first) | (block_of(source) == second), factor * drawn, drawn)


def levels(key, extent, shards, least, high):
    def one(axis_at, shards_of):
        steps = jax.random.uniform(jax.random.fold_in(jax.random.fold_in(key, 6), axis_at), (shards_of,), jnp.float32, least / len(shards), high / len(shards))
        return jnp.repeat(jnp.exp(steps), extent[axis_at] // shards_of).reshape((-1,) + (1,) * (len(extent) - axis_at - 1))

    factor_of = one(*shards[0])
    for cut in shards[1:]:
        factor_of = factor_of * one(*cut)
    return factor_of


def centred(own_key, extent, width, reach, cuts=(), kind=jnp.bfloat16):
    loudness = levels(own_key, extent, cuts, -0.22, 0.18) if cuts else 1.0
    values = jax.random.normal(own_key, extent, jnp.float32) * width * loudness
    return jnp.minimum(jnp.maximum(values, -reach), reach).astype(kind)


def gaussian_with(stream_key, extent, spread, limit, cuts, heavy, kind=jnp.bfloat16):
    values = spread * jax.random.normal(stream_key, extent, jnp.float32)
    if cuts:
        values = values * levels(stream_key, extent, cuts, -0.22, 0.18)
    return jnp.clip(raised(values, jax.random.fold_in(stream_key, 3), *heavy), -limit, limit).astype(kind)


def setup_inputs(seed: int = 0) -> dict:
    streams_of = jax.random.split(jax.random.key(seed), 6)
    return {
        "panel": centred(streams_of[0], (N, K), 1.0, 6.0, ((0, 64), (1, 4))),
        "basis": gaussian_with(streams_of[1], (N, Q), N ** -0.5, 0.03125, ((0, 64), (1, 4)), (0, 1, 64, 4.0)),
        "g_blocks": centred(streams_of[2], (NB, SLOTS, BS, BS), (SLOTS * BS) ** -0.5, 0.3125, ((0, 64),)),
        "c_blocks": centred(streams_of[3], (NB, SLOTS, BS, BS), (SLOTS * BS) ** -0.5, 0.3125, ((0, 64),)),
        "block_cols": draw_block_cols(jax.random.fold_in(streams_of[5], 71), 0),
    }


def multiply(blocks, pieces, block_cols):
    block_rows = pieces.shape[0]
    summed = jnp.zeros(pieces.shape, jnp.float32)
    for slot_idx in range(SLOTS):
        nearby = pieces[block_cols[:, slot_idx]].astype(jnp.float32)
        summed = summed + jnp.einsum('rab,rbk->rak', blocks[:, slot_idx].astype(jnp.float32), nearby)
    return summed.reshape(block_rows * pieces.shape[1], pieces.shape[2]).astype(jnp.bfloat16)


def reference(panel, basis, g_blocks, c_blocks, block_cols):
    block_rows = block_cols.shape[0]
    pieces = panel.reshape(block_rows, g_blocks.shape[2], panel.shape[1])
    y_g = multiply(g_blocks, pieces, block_cols)
    y_c = multiply(c_blocks, pieces, block_cols)
    dims = (((0,), (0,)), ((), ()))
    reduced_g = lax.dot_general(basis, y_g, dims, preferred_element_type=jnp.float32)
    reduced_c = lax.dot_general(basis, y_c, dims, preferred_element_type=jnp.float32)
    return (reduced_g, reduced_c)
```

```python
import functools

import jax
import jax.numpy as jnp
from jax import lax
from jax.experimental import pallas as pl
from jax.experimental.pallas import tpu as pltpu
from jax.sharding import PartitionSpec as P

BS = 128
HB = 4
MESH = pl.DeviceIdType.MESH
F32, BF16 = jnp.float32, jnp.bfloat16
INNER = (4, 13, 22, 29, 34)
ROW_UNROLL = 2


def span(first, last):
    return pl.ds(first * BS, (last - first) * BS)


def kernel(
    nodes, xt, basis, gb, cb, bc, outg, outc,
    xl, xr, wl, w0, w1, w2, w3, gv, cv, bv, yt, acc, stage, land,
    lsem, ssem, rsem, sum_send, sum_recv,
):
    nb = gb.shape[0]
    width = xt.shape[0]
    node, col = lax.axis_index("node"), lax.axis_index("col")
    core, x_lo = lax.rem(col, 2), col // 2
    y, z, x_hi = lax.rem(node, 4), lax.rem(node // 4, 8), node // 32
    above = (lax.rem(node + 1, nodes), col)
    below = (lax.rem(node + nodes - 1, nodes), col)
    across = (node, lax.rem(col + 2, 4))
    beside = (node, col + 1 - 2 * core)
    mine = pl.ds(pl.multiple_of(core * width, width), width)

    loads = [pltpu.make_async_copy(xt, xl.at[mine, span(HB, HB + nb)], lsem.at[0])]
    half = nb // 2
    for k, (src, dst) in enumerate(((gb, gv), (cb, cv))):
        for part in range(2):
            rows = pl.ds(part * half, half)
            loads.append(pltpu.make_async_copy(src.at[rows], dst.at[rows], lsem.at[1 + 2 * part + k]))
    loads.append(pltpu.make_async_copy(basis, bv, lsem.at[5]))
    for load in (loads[0], loads[1], loads[3], loads[2], loads[4], loads[5]):
        load.start()

    barrier = pltpu.get_barrier_semaphore()

    def greet(k, carry):
        pl.semaphore_signal(barrier, inc=1, device_id=(lax.rem(node + k, nodes), col), device_id_type=MESH)
        return carry

    pl.semaphore_signal(barrier, inc=1, device_id=across, device_id_type=MESH)
    pl.semaphore_signal(barrier, inc=1, device_id=beside, device_id_type=MESH)
    lax.fori_loop(1, nodes, greet, 0)
    pl.semaphore_wait(barrier, nodes + 1)

    made = []

    def remote(src, dst, device):
        k = len(made)
        made.append(
            pltpu.make_async_remote_copy(
                src_ref=src, dst_ref=dst, send_sem=ssem.at[k], recv_sem=rsem.at[k],
                device_id=device, device_id_type=MESH,
            )
        )
        return made[-1]

    chunks = [(0, HB), (nb - HB, nb)] + list(zip(INNER[:-1], INNER[1:]))
    lo, hi = span(0, HB), span(nb - HB, nb)
    halo_lo, halo_hi = span(0, HB), span(nb + HB, nb + 2 * HB)

    cross = [remote(xt.at[:, span(a, b)], xr.at[mine, span(a + HB, b + HB)], across) for a, b in chunks]
    pass_on = [
        remote(xr.at[mine, span(a + HB, b + HB)], xr.at[mine, span(a + HB, b + HB)], beside) for a, b in chunks
    ]
    own_up = remote(xt.at[:, hi], xl.at[mine, halo_lo], above)
    own_down = remote(xt.at[:, lo], xl.at[mine, halo_hi], below)
    own_body = remote(xt, xl.at[mine, span(HB, HB + nb)], beside)
    own_lo = remote(xl.at[mine, halo_lo], xl.at[mine, halo_lo], beside)
    own_hi = remote(xl.at[mine, halo_hi], xl.at[mine, halo_hi], beside)
    far_up = remote(xr.at[mine, span(nb, nb + HB)], xr.at[mine, halo_lo], above)
    far_down = remote(xr.at[mine, span(HB, 2 * HB)], xr.at[mine, halo_hi], below)
    far_lo = remote(xr.at[mine, halo_lo], xr.at[mine, halo_lo], beside)
    far_hi = remote(xr.at[mine, halo_hi], xr.at[mine, halo_hi], beside)

    for copy in (cross[0], cross[1], own_up, own_down, *cross[2:], own_body):
        copy.start()

    def fill(window, slices, shift):
        for b in range(window.shape[0]):
            window[b] = slices[:, span(b + shift, b + shift + 1)]

    def products(window, first, last, shift):
        def tile(s, i):
            return window[jnp.clip(bc[s, i] - (node * nb - HB + shift), 0, window.shape[0] - 1)]

        def row(i):
            tiles = [tile(s, i) for s in range(3)]
            rhs = jnp.concatenate(
                [jnp.concatenate([m[i, s] for s in range(3)], axis=1) for m in (gv, cv)], axis=0
            )
            made_rows = lax.dot_general(
                jnp.concatenate(tiles, axis=1), rhs, (((1,), (1,)), ((), ())), preferred_element_type=F32
            ).astype(BF16)
            at = pl.ds(pl.multiple_of(i * BS, BS), BS)
            yt[: 2 * width, at] = made_rows[:, :BS]
            yt[2 * width :, at] = made_rows[:, BS:]

        count = last - first
        steps = count // ROW_UNROLL

        def several(k, carry):
            for u in range(ROW_UNROLL):
                row(first + k * ROW_UNROLL + u)
            return carry

        lax.fori_loop(0, steps, several, 0)
        for i in range(first + steps * ROW_UNROLL, last):
            row(i)

    def project(first, last, fresh):
        rows = span(first, last)
        part = jnp.dot(yt[:, rows], bv[rows, :], preferred_element_type=F32)
        acc[...] = part if fresh else acc[...] + part

    def place(k):
        to_x = lax.rem(x_hi + 1 - k // 32, 2)
        to_z = lax.rem(z + lax.rem(k // 4, 8) + 4, 8)
        to_y = lax.rem(y + lax.rem(k, 4) + 2, 4)
        return (to_x * 8 + to_z) * 4 + to_y

    own_k = 32 + 4 * 4 + 2

    def scatter(which):
        for s in range(acc.shape[1] // BS):
            turned = acc[:, s * BS : (s + 1) * BS].T.astype(BF16)
            stage[which, s * 16 : (s + 1) * 16] = turned.reshape(16, 8, acc.shape[0])

        def send(slot, k):
            to = place(k)
            pltpu.make_async_remote_copy(
                src_ref=stage.at[which, to], dst_ref=land.at[which, slot],
                send_sem=sum_send.at[which], recv_sem=sum_recv.at[which],
                device_id=(to, col), device_id_type=MESH,
            ).start()

        def early(k, carry):
            send(k, k)
            return carry

        def late(k, carry):
            send(k - 1, k)
            return carry

        lax.fori_loop(0, own_k, early, 0)
        lax.fori_loop(own_k + 1, nodes, late, 0)

    def all_sums(which):
        return pltpu.make_async_remote_copy(
            src_ref=stage.at[which, pl.ds(0, nodes - 1)], dst_ref=land.at[which, pl.ds(0, nodes - 1)],
            send_sem=sum_send.at[which], recv_sem=sum_recv.at[which],
            device_id=across, device_id_type=MESH,
        )

    def gather_sums(which, at):
        all_sums(which).wait_recv()
        total = stage[which, node].astype(F32)
        for k in range(nodes - 1):
            total = total + land[which, k].astype(F32)
        outg[:, at] = total[:, : 2 * width]
        outc[:, at] = total[:, 2 * width :]

    own_up.wait_recv()
    own_lo.start()
    own_down.wait_recv()
    own_hi.start()
    cross[0].wait_recv()
    pass_on[0].start()
    far_down.start()
    cross[1].wait_recv()
    pass_on[1].start()
    far_up.start()
    loads[0].wait()
    own_body.wait_recv()
    own_lo.wait_recv()
    own_hi.wait_recv()

    loads[1].wait()
    loads[3].wait()
    fill(wl, xl, 0)
    products(wl, 0, half, 0)
    cross[2].wait_recv()
    pass_on[2].start()
    far_up.wait_recv()
    far_lo.start()
    far_down.wait_recv()
    far_hi.start()
    loads[2].wait()
    loads[4].wait()
    products(wl, half, nb, 0)
    loads[5].wait()
    project(0, half, True)
    cross[3].wait_recv()
    pass_on[3].start()
    project(half, nb, False)
    scatter(0)

    far_lo.wait_recv()
    far_hi.wait_recv()
    pass_on[0].wait_recv()
    pass_on[1].wait_recv()
    ends = [b - HB for b in INNER[1:-1]] + [nb]
    starts = [0] + ends[:-1]
    for p, (window, a, b) in enumerate(zip((w0, w1, w2, w3), starts, ends)):
        if p >= 2:
            cross[2 + p].wait_recv()
            pass_on[2 + p].start()
        pass_on[2 + p].wait_recv()
        fill(window, xr, a)
        products(window, a, b, a)
        project(a, b, p == 0)
    scatter(1)

    near_at = pl.ds(pl.multiple_of(x_lo * 2 * width, 2 * width), 2 * width)
    far_at = pl.ds(pl.multiple_of((1 - x_lo) * 2 * width, 2 * width), 2 * width)
    gather_sums(0, near_at)
    gather_sums(1, far_at)
    for copy in made:
        copy.wait_send()
    for which in range(2):
        all_sums(which).wait_send()


def body(panel, basis, g_blocks, c_blocks, block_cols):
    nodes = lax.axis_size("node")
    nb = g_blocks.shape[0]
    width, states = panel.shape[1], basis.shape[1]
    ext = (nb + 2 * HB) * BS
    ends = [b - HB for b in INNER[1:-1]] + [nb]
    starts = [0] + ends[:-1]
    any_spec = pl.BlockSpec(memory_space=pl.ANY)
    vmem_spec = pl.BlockSpec(memory_space=pltpu.VMEM)
    reduced = jax.ShapeDtypeStruct((states // nodes, 4 * width), F32)
    return pl.pallas_call(
        functools.partial(kernel, nodes),
        out_shape=(reduced, reduced),
        in_specs=[any_spec] * 4 + [pl.BlockSpec(memory_space=pltpu.SMEM)],
        out_specs=(vmem_spec, vmem_spec),
        scratch_shapes=[
            pltpu.VMEM((2 * width, ext), BF16),
            pltpu.VMEM((2 * width, ext), BF16),
            *[pltpu.VMEM((b - a + 2 * HB, 2 * width, BS), BF16) for a, b in zip([0] + starts, [nb] + ends)],
            pltpu.VMEM(g_blocks.shape, BF16),
            pltpu.VMEM(c_blocks.shape, BF16),
            pltpu.VMEM(basis.shape, BF16),
            pltpu.VMEM((4 * width, nb * BS), BF16),
            pltpu.VMEM((4 * width, states), F32),
            pltpu.VMEM((2, nodes, states // nodes, 4 * width), BF16),
            pltpu.VMEM((2, nodes, states // nodes, 4 * width), BF16),
            pltpu.SemaphoreType.DMA((6,)),
            pltpu.SemaphoreType.DMA((24,)),
            pltpu.SemaphoreType.DMA((24,)),
            pltpu.SemaphoreType.DMA((2,)),
            pltpu.SemaphoreType.DMA((2,)),
        ],
        compiler_params=pltpu.CompilerParams(
            collective_id=0, has_side_effects=True, vmem_limit_bytes=61 << 20
        ),
        name="project",
    )(panel.T, basis, g_blocks, c_blocks, block_cols.T)


def solution(mesh):
    in_specs = (
        P("node", "col"),
        P("node", "col"),
        P("node", None, None, None),
        P("node", None, None, None),
        P("node", None),
    )
    out_specs = (P(("col", "node"), None), P(("col", "node"), None))
    return jax.shard_map(body, mesh=mesh, in_specs=in_specs, out_specs=out_specs, check_vma=False)
```

```python
import functools

import jax
import jax.numpy as jnp
from jax import lax
from jax.experimental import pallas as pl
from jax.experimental.pallas import tpu as pltpu
from jax.sharding import PartitionSpec as P

BS = 128
HB = 4
MESH = pl.DeviceIdType.MESH
F32, BF16 = jnp.float32, jnp.bfloat16
INNER = (4, 13, 22, 32, 34)
ROW_UNROLL = 15


def span(first, last):
    return pl.ds(first * BS, (last - first) * BS)


def kernel(
    nodes, xt, basis, gb, cb, bc, out,
    xl, xr, wi, we, wf, w0, w1, w2, w3, gv, cv, bv, yt, acc, stage, land,
    lsem, ssem, rsem, sum_send, sum_recv,
):
    nb = gb.shape[0]
    width = xt.shape[0]
    node, col = lax.axis_index("node"), lax.axis_index("col")
    core, x_lo = lax.rem(col, 2), col // 2
    y, z, x_hi = lax.rem(node, 4), lax.rem(node // 4, 8), node // 32
    above = (lax.rem(node + 1, nodes), col)
    below = (lax.rem(node + nodes - 1, nodes), col)
    across = (node, lax.rem(col + 2, 4))
    beside = (node, col + 1 - 2 * core)
    diagonal = (node, lax.rem(col + 2, 4) + 1 - 2 * core)
    mine = pl.ds(pl.multiple_of(core * width, width), width)

    loads = [pltpu.make_async_copy(xt, xl.at[mine, span(HB, HB + nb)], lsem.at[0])]
    half = nb // 2
    for k, (src, dst) in enumerate(((gb, gv), (cb, cv))):
        for part in range(2):
            rows = pl.ds(part * half, half)
            loads.append(pltpu.make_async_copy(src.at[rows], dst.at[rows], lsem.at[1 + 2 * part + k]))
    loads.append(pltpu.make_async_copy(basis, bv, lsem.at[5]))
    for load in (loads[0], loads[1], loads[3], loads[2], loads[4], loads[5]):
        load.start()

    barrier = pltpu.get_barrier_semaphore()

    def greet(k, carry):
        pl.semaphore_signal(barrier, inc=1, device_id=(lax.rem(node + k, nodes), col), device_id_type=MESH)
        return carry

    for near in (across, beside, diagonal):
        pl.semaphore_signal(barrier, inc=1, device_id=near, device_id_type=MESH)
    lax.fori_loop(1, nodes, greet, 0)
    pl.semaphore_wait(barrier, nodes + 2)

    made = []

    def remote(src, dst, device):
        k = len(made)
        made.append(
            pltpu.make_async_remote_copy(
                src_ref=src, dst_ref=dst, send_sem=ssem.at[k], recv_sem=rsem.at[k],
                device_id=device, device_id_type=MESH,
            )
        )
        return made[-1]

    chunks = [(0, HB), (nb - HB, nb)] + list(zip(INNER[:-1], INNER[1:]))
    lo, hi = span(0, HB), span(nb - HB, nb)
    halo_lo, halo_hi = span(0, HB), span(nb + HB, nb + 2 * HB)

    cross = [remote(xt.at[:, span(a, b)], xr.at[mine, span(a + HB, b + HB)], across) for a, b in chunks]
    pass_on = [
        remote(xr.at[mine, span(a + HB, b + HB)], xr.at[mine, span(a + HB, b + HB)], beside) for a, b in chunks[:-1]
    ]
    last = span(*chunks[-1])
    cross_both = remote(xt.at[:, last], xr.at[mine, span(INNER[-2] + HB, INNER[-1] + HB)], diagonal)
    own_up = remote(xt.at[:, hi], xl.at[mine, halo_lo], above)
    own_down = remote(xt.at[:, lo], xl.at[mine, halo_hi], below)
    own_body = remote(xt, xl.at[mine, span(HB, HB + nb)], beside)
    own_lo = remote(xl.at[mine, halo_lo], xl.at[mine, halo_lo], beside)
    own_hi = remote(xl.at[mine, halo_hi], xl.at[mine, halo_hi], beside)
    far_up = remote(xr.at[mine, span(nb, nb + HB)], xr.at[mine, halo_lo], above)
    far_down = remote(xr.at[mine, span(HB, 2 * HB)], xr.at[mine, halo_hi], below)
    far_lo = remote(xr.at[mine, halo_lo], xr.at[mine, halo_lo], beside)
    far_hi = remote(xr.at[mine, halo_hi], xr.at[mine, halo_hi], beside)

    for copy in (cross[0], cross[1], own_up, own_down, own_body, *cross[2:], cross_both):
        copy.start()

    def fill(window, slices, shift):
        for b in range(window.shape[0]):
            window[b] = slices[:, span(b + shift, b + shift + 1)]

    def products(window, first, last, shift):
        def tile(s, i):
            return window[jnp.clip(bc[s, i] - (node * nb - HB + shift), 0, window.shape[0] - 1)]

        def row(i):
            tiles = [tile(s, i) for s in range(3)]
            rhs = jnp.concatenate(
                [jnp.concatenate([m[i, s] for s in range(3)], axis=1) for m in (gv, cv)], axis=0
            )
            made_rows = lax.dot_general(
                jnp.concatenate(tiles, axis=1), rhs, (((1,), (1,)), ((), ())), preferred_element_type=F32
            ).astype(BF16)
            at = pl.ds(pl.multiple_of(i * BS, BS), BS)
            yt[: 2 * width, at] = made_rows[:, :BS]
            yt[2 * width :, at] = made_rows[:, BS:]

        count = last - first
        steps = count // ROW_UNROLL if count > ROW_UNROLL else 0

        def several(k, carry):
            for u in range(ROW_UNROLL):
                row(first + k * ROW_UNROLL + u)
            return carry

        if steps:
            lax.fori_loop(0, steps, several, 0)
        for i in range(first + steps * ROW_UNROLL, last):
            row(i)

    def project(first, last, fresh):
        rows = span(first, last)
        part = jnp.dot(yt[:, rows], bv[rows, :], preferred_element_type=F32)
        acc[...] = part if fresh else acc[...] + part

    to_x = [lax.rem(x_hi + d, 2) * 32 for d in (1, 0)]
    to_z = [lax.rem(z + d, 8) * 4 for d in (4, 3, 5, 2, 6, 1, 7, 0)]
    to_y = [lax.rem(y + d, 4) for d in (2, 1, 3, 0)]
    owners = [tx + tz + ty for tz in to_z for tx in to_x for ty in to_y][:-1]

    def scatter(which):
        for s in range(acc.shape[1] // BS):
            turned = acc[:, s * BS : (s + 1) * BS].T.astype(BF16)
            stage[which, s * 16 : (s + 1) * 16] = turned.reshape(16, 8, acc.shape[0])
        for slot, to in enumerate(owners):
            pltpu.make_async_remote_copy(
                src_ref=stage.at[which, to], dst_ref=land.at[which, slot],
                send_sem=sum_send.at[which], recv_sem=sum_recv.at[which],
                device_id=(to, col), device_id_type=MESH,
            ).start()

    def all_sums(which):
        return pltpu.make_async_remote_copy(
            src_ref=stage.at[which, pl.ds(0, nodes - 1)], dst_ref=land.at[which, pl.ds(0, nodes - 1)],
            send_sem=sum_send.at[which], recv_sem=sum_recv.at[which],
            device_id=across, device_id_type=MESH,
        )

    def gather_sums(which, at):
        all_sums(which).wait_recv()
        total = stage[which, node].astype(F32)
        for k in range(nodes - 1):
            total = total + land[which, k].astype(F32)
        out[0, :, at] = total[:, : 2 * width]
        out[1, :, at] = total[:, 2 * width :]

    own_up.wait_recv()
    own_lo.start()
    own_down.wait_recv()
    own_hi.start()

    loads[0].wait()
    own_body.wait_recv()
    fill(wi, xl, HB)
    for load in loads[1:5]:
        load.wait()
    products(wi, HB, nb - HB, HB)
    cross[0].wait_recv()
    pass_on[0].start()
    far_down.start()
    cross[1].wait_recv()
    pass_on[1].start()
    far_up.start()
    own_lo.wait_recv()
    fill(we, xl, 0)
    products(we, 0, HB, 0)
    own_hi.wait_recv()
    fill(wf, xl, nb - HB)
    products(wf, nb - HB, nb, nb - HB)
    cross[2].wait_recv()
    pass_on[2].start()
    loads[5].wait()
    project(0, nb, True)
    far_up.wait_recv()
    far_lo.start()
    far_down.wait_recv()
    far_hi.start()
    cross[3].wait_recv()
    pass_on[3].start()
    scatter(0)

    ends = [b - HB for b in INNER[1:-1]] + [nb]
    starts = [0] + ends[:-1]
    far_lo.wait_recv()
    pass_on[0].wait_recv()
    for p, (window, a, b) in enumerate(zip((w0, w1, w2, w3), starts, ends)):
        if p < 3:
            pass_on[2 + p].wait_recv()
        else:
            far_hi.wait_recv()
            pass_on[1].wait_recv()
            cross[5].wait_recv()
            cross_both.wait_recv()
        fill(window, xr, a)
        products(window, a, b, a)
        project(a, b, p == 0)
        if p == 1:
            cross[4].wait_recv()
            pass_on[4].start()
    scatter(1)

    near_at = pl.ds(pl.multiple_of(x_lo * 2 * width, 2 * width), 2 * width)
    far_at = pl.ds(pl.multiple_of((1 - x_lo) * 2 * width, 2 * width), 2 * width)
    gather_sums(0, near_at)
    gather_sums(1, far_at)
    for copy in made:
        copy.wait_send()
    for which in range(2):
        all_sums(which).wait_send()


def body(panel, basis, g_blocks, c_blocks, block_cols):
    nodes = lax.axis_size("node")
    nb = g_blocks.shape[0]
    width, states = panel.shape[1], basis.shape[1]
    ext = (nb + 2 * HB) * BS
    ends = [b - HB for b in INNER[1:-1]] + [nb]
    starts = [0] + ends[:-1]
    any_spec = pl.BlockSpec(memory_space=pl.ANY)
    vmem_spec = pl.BlockSpec(memory_space=pltpu.VMEM)
    windows = [(HB, nb - HB), (0, HB), (nb - HB, nb), *zip(starts, ends)]
    reduced = pl.pallas_call(
        functools.partial(kernel, nodes),
        out_shape=jax.ShapeDtypeStruct((2, states // nodes, 4 * width), F32),
        in_specs=[any_spec] * 4 + [pl.BlockSpec(memory_space=pltpu.SMEM)],
        out_specs=vmem_spec,
        scratch_shapes=[
            pltpu.VMEM((2 * width, ext), BF16),
            pltpu.VMEM((2 * width, ext), BF16),
            *[pltpu.VMEM((b - a + 2 * HB, 2 * width, BS), BF16) for a, b in windows],
            pltpu.VMEM(g_blocks.shape, BF16),
            pltpu.VMEM(c_blocks.shape, BF16),
            pltpu.VMEM(basis.shape, BF16),
            pltpu.VMEM((4 * width, nb * BS), BF16),
            pltpu.VMEM((4 * width, states), F32),
            pltpu.VMEM((2, nodes, states // nodes, 4 * width), BF16),
            pltpu.VMEM((2, nodes, states // nodes, 4 * width), BF16),
            pltpu.SemaphoreType.DMA((6,)),
            pltpu.SemaphoreType.DMA((24,)),
            pltpu.SemaphoreType.DMA((24,)),
            pltpu.SemaphoreType.DMA((2,)),
            pltpu.SemaphoreType.DMA((2,)),
        ],
        compiler_params=pltpu.CompilerParams(
            collective_id=0, has_side_effects=True, vmem_limit_bytes=61 << 20
        ),
        name="project",
    )(panel.T, basis, g_blocks, c_blocks, block_cols.T)
    return reduced[0], reduced[1]


def solution(mesh):
    in_specs = (
        P("node", "col"),
        P("node", "col"),
        P("node", None, None, None),
        P("node", None, None, None),
        P("node", None),
    )
    out_specs = (P(("col", "node"), None), P(("col", "node"), None))
    return jax.shard_map(body, mesh=mesh, in_specs=in_specs, out_specs=out_specs, check_vma=False)
```

```python
import functools

import jax
import jax.numpy as jnp
from jax import lax
from jax.experimental import pallas as pl
from jax.experimental.pallas import tpu as pltpu
from jax.sharding import PartitionSpec as P

BS = 128
HB = 4
MESH = pl.DeviceIdType.MESH
F32, BF16 = jnp.float32, jnp.bfloat16
INNER = (4, 15, 26, 32, 34)
ROW_UNROLL = 15


def span(first, last):
    return pl.ds(first * BS, (last - first) * BS)


def kernel(
    nodes, xt, basis, gb, cb, bc, out,
    xl, xr, wi, we, wf, w0, w1, w2, w3, gv, cv, bv, yt, acc,
    stage, land, first, first_in, second, second_in, lsem, ssem, rsem, sum_send, sum_recv, part_send, part_recv, known,
):
    nb = gb.shape[0]
    width = xt.shape[0]
    node, col = lax.axis_index("node"), lax.axis_index("col")
    core, x_lo = lax.rem(col, 2), col // 2
    y, z, x_hi = lax.rem(node, 4), lax.rem(node // 4, 8), node // 32
    above = (lax.rem(node + 1, nodes), col)
    below = (lax.rem(node + nodes - 1, nodes), col)
    above_beside = (above[0], col + 1 - 2 * core)
    below_beside = (below[0], col + 1 - 2 * core)
    across = (node, lax.rem(col + 2, 4))
    beside = (node, col + 1 - 2 * core)
    diagonal = (node, lax.rem(col + 2, 4) + 1 - 2 * core)
    mine = pl.ds(pl.multiple_of(core * width, width), width)

    loads = [pltpu.make_async_copy(xt, xl.at[mine, span(HB, HB + nb)], lsem.at[0])]
    half = nb // 2
    for k, (src, dst) in enumerate(((gb, gv), (cb, cv))):
        for part in range(2):
            rows = pl.ds(part * half, half)
            loads.append(pltpu.make_async_copy(src.at[rows], dst.at[rows], lsem.at[1 + 2 * part + k]))
    loads.append(pltpu.make_async_copy(basis, bv, lsem.at[5]))
    for load in (loads[0], loads[1], loads[3], loads[2], loads[4], loads[5]):
        load.start()

    barrier = pltpu.get_barrier_semaphore()
    y_line = [(node - y + lax.rem(y + d, 4), col) for d in (1, 2, 3)]
    z_line = [((x_hi * 8 + lax.rem(z + d, 8)) * 4 + y, col) for d in range(1, 8)]
    near = [across, beside, diagonal, (lax.rem(node + nodes // 2, nodes), col)] + y_line + z_line

    def greet(device):
        pl.semaphore_signal(barrier, inc=1, device_id=device, device_id_type=MESH)

    for peer in near:
        greet(peer)
    for peer in (above, below, above_beside, below_beside):
        greet(peer)
    pl.semaphore_wait(barrier, len(near) + 4)

    def tell(r):
        for peer in (y_line, z_line)[r]:
            pl.semaphore_signal(known.at[r], inc=1, device_id=peer, device_id_type=MESH)

    def hear(r):
        pl.semaphore_wait(known.at[r], len((y_line, z_line)[r]))

    made = []

    def remote(src, dst, device):
        k = len(made)
        made.append(
            pltpu.make_async_remote_copy(
                src_ref=src, dst_ref=dst, send_sem=ssem.at[k], recv_sem=rsem.at[k],
                device_id=device, device_id_type=MESH,
            )
        )
        return made[-1]

    chunks = [(0, HB), (nb - HB, nb)] + list(zip(INNER[:-1], INNER[1:]))
    lo, hi = span(0, HB), span(nb - HB, nb)
    halo_lo, halo_hi = span(0, HB), span(nb + HB, nb + 2 * HB)

    cross = [remote(xt.at[:, span(a, b)], xr.at[mine, span(a + HB, b + HB)], across) for a, b in chunks]
    pass_on = [
        remote(xr.at[mine, span(a + HB, b + HB)], xr.at[mine, span(a + HB, b + HB)], beside) for a, b in chunks[:-1]
    ]
    last = span(*chunks[-1])
    cross_both = remote(xt.at[:, last], xr.at[mine, span(INNER[-2] + HB, INNER[-1] + HB)], diagonal)
    own_up = [remote(xt.at[:, hi], xl.at[mine, halo_lo], to) for to in (above, above_beside)]
    own_down = [remote(xt.at[:, lo], xl.at[mine, halo_hi], to) for to in (below, below_beside)]
    own_body = remote(xt, xl.at[mine, span(HB, HB + nb)], beside)
    far_up = [remote(xr.at[mine, span(nb, nb + HB)], xr.at[mine, halo_lo], to) for to in (above, above_beside)]
    far_down = [remote(xr.at[mine, span(HB, 2 * HB)], xr.at[mine, halo_hi], to) for to in (below, below_beside)]

    for copy in (cross[0], cross[1], own_body, *own_up, *own_down, *cross[2:], cross_both):
        copy.start()

    def fill(window, slices, shift):
        for b in range(window.shape[0]):
            window[b] = slices[:, span(b + shift, b + shift + 1)]

    def products(window, first, last, shift):
        def tile(s, i):
            return window[jnp.clip(bc[s, i] - (node * nb - HB + shift), 0, window.shape[0] - 1)]

        def row(i):
            tiles = [tile(s, i) for s in range(3)]
            rhs = jnp.concatenate(
                [jnp.concatenate([m[i, s] for s in range(3)], axis=1) for m in (gv, cv)], axis=0
            )
            made_rows = lax.dot_general(
                jnp.concatenate(tiles, axis=1), rhs, (((1,), (1,)), ((), ())), preferred_element_type=F32
            ).astype(BF16)
            at = pl.ds(pl.multiple_of(i * BS, BS), BS)
            yt[: 2 * width, at] = made_rows[:, :BS]
            yt[2 * width :, at] = made_rows[:, BS:]

        count = last - first
        steps = count // ROW_UNROLL if count > ROW_UNROLL else 0

        def several(k, carry):
            for u in range(ROW_UNROLL):
                row(first + k * ROW_UNROLL + u)
            return carry

        if steps:
            lax.fori_loop(0, steps, several, 0)
        for i in range(first + steps * ROW_UNROLL, last):
            row(i)

    def project(first, last, fresh):
        rows = span(first, last)
        part = jnp.dot(yt[:, rows], bv[rows, :], preferred_element_type=F32)
        acc[...] = part if fresh else acc[...] + part

    to_x = [lax.rem(x_hi + d, 2) * 32 for d in (1, 0)]
    to_z = [lax.rem(z + d, 8) * 4 for d in (4, 3, 5, 2, 6, 1, 7, 0)]
    to_y = [lax.rem(y + d, 4) for d in (2, 1, 3, 0)]
    owners = [tx + tz + ty for tz in to_z for tx in to_x for ty in to_y][:-1]

    along_y = [
        pltpu.make_async_remote_copy(
            src_ref=first.at[to], dst_ref=first_in.at[k], send_sem=part_send.at[k], recv_sem=part_recv.at[k],
            device_id=(node - y + to, col), device_id_type=MESH,
        )
        for k, to in enumerate(to_y[:3])
    ]
    lines = [tx // 4 + tz // 4 for tz in to_z for tx in to_x]
    along_zx = [
        pltpu.make_async_remote_copy(
            src_ref=second.at[to], dst_ref=second_in.at[k], send_sem=part_send.at[3 + k], recv_sem=part_recv.at[3 + k],
            device_id=(to * 4 + y, col), device_id_type=MESH,
        )
        for k, to in enumerate(lines[:-1])
    ]

    def turned(s):
        return acc[:, s * BS : (s + 1) * BS].T.astype(BF16)

    def scatter_first():
        for s in range(acc.shape[1] // BS):
            tile = turned(s).reshape(4, 4, 8, acc.shape[0])
            for to in range(4):
                first[to, 4 * s : 4 * s + 4] = tile[:, to]
        for copy in along_y:
            copy.start()

    def pass_first():
        for copy in along_y:
            copy.wait_recv()
        for half_of in range(2):
            some = pl.ds(half_of * 8, 8)
            total = first[y, some].astype(F32)
            for k in range(3):
                total = total + first_in[k, some].astype(F32)
            second[some] = total.astype(BF16)
        for copy in along_zx:
            copy.start()

    def scatter_second():
        for s in range(acc.shape[1] // BS):
            stage[s * 16 : (s + 1) * 16] = turned(s).reshape(16, 8, acc.shape[0])
        for slot, to in enumerate(owners):
            pltpu.make_async_remote_copy(
                src_ref=stage.at[to], dst_ref=land.at[slot], send_sem=sum_send, recv_sem=sum_recv,
                device_id=(to, col), device_id_type=MESH,
            ).start()

    all_sums = pltpu.make_async_remote_copy(
        src_ref=stage.at[pl.ds(0, nodes - 1)], dst_ref=land, send_sem=sum_send, recv_sem=sum_recv,
        device_id=across, device_id_type=MESH,
    )

    def write(total, half_at):
        at = pl.ds(pl.multiple_of(half_at * 2 * width, 2 * width), 2 * width)
        out[0, :, at] = total[:, : 2 * width]
        out[1, :, at] = total[:, 2 * width :]

    def land_all(copies):
        for copy in copies:
            copy.wait_recv()

    tell(0)

    loads[0].wait()
    own_body.wait_recv()
    fill(wi, xl, HB)
    for load in loads[1:5]:
        load.wait()
    products(wi, HB, nb // 2, HB)
    cross[0].wait_recv()
    pass_on[0].start()
    for copy in far_down:
        copy.start()
    cross[1].wait_recv()
    pass_on[1].start()
    for copy in far_up:
        copy.start()
    hear(0)
    tell(1)
    products(wi, nb // 2, nb - HB, HB)
    land_all(own_up)
    fill(we, xl, 0)
    products(we, 0, HB, 0)
    land_all(own_down)
    fill(wf, xl, nb - HB)
    products(wf, nb - HB, nb, nb - HB)
    cross[2].wait_recv()
    pass_on[2].start()
    loads[5].wait()
    project(0, nb, True)
    scatter_first()

    ends = [b - HB for b in INNER[1:-1]] + [nb]
    starts = [0] + ends[:-1]
    needs = (far_up + [pass_on[0], pass_on[2]], [pass_on[3]], [pass_on[4]], far_down + [pass_on[1], cross[5], cross_both])
    for p, (window, a, b) in enumerate(zip((w0, w1, w2, w3), starts, ends)):
        land_all(needs[p])
        fill(window, xr, a)
        products(window, a, b, a)
        project(a, b, p == 0)
        if p < 2:
            cross[3 + p].wait_recv()
            pass_on[3 + p].start()
        if p == 0:
            hear(1)
            pass_first()
    scatter_second()

    total = second[node // 4].astype(F32)
    for k, copy in enumerate(along_zx):
        copy.wait_recv()
        total = total + second_in[k].astype(F32)
    write(total, x_lo)
    all_sums.wait_recv()
    total = stage[node].astype(F32)
    for k in range(nodes - 1):
        total = total + land[k].astype(F32)
    write(total, 1 - x_lo)
    for copy in (*made, *along_y, *along_zx, all_sums):
        copy.wait_send()


def body(panel, basis, g_blocks, c_blocks, block_cols):
    nodes = lax.axis_size("node")
    nb = g_blocks.shape[0]
    width, states = panel.shape[1], basis.shape[1]
    ext = (nb + 2 * HB) * BS
    ends = [b - HB for b in INNER[1:-1]] + [nb]
    starts = [0] + ends[:-1]
    piece = (states // nodes, 4 * width)
    any_spec = pl.BlockSpec(memory_space=pl.ANY)
    vmem_spec = pl.BlockSpec(memory_space=pltpu.VMEM)
    windows = [(HB, nb - HB), (0, HB), (nb - HB, nb), *zip(starts, ends)]
    reduced = pl.pallas_call(
        functools.partial(kernel, nodes),
        out_shape=jax.ShapeDtypeStruct((2, *piece), F32),
        in_specs=[any_spec] * 4 + [pl.BlockSpec(memory_space=pltpu.SMEM)],
        out_specs=vmem_spec,
        scratch_shapes=[
            pltpu.VMEM((2 * width, ext), BF16),
            pltpu.VMEM((2 * width, ext), BF16),
            *[pltpu.VMEM((b - a + 2 * HB, 2 * width, BS), BF16) for a, b in windows],
            pltpu.VMEM(g_blocks.shape, BF16),
            pltpu.VMEM(c_blocks.shape, BF16),
            pltpu.VMEM(basis.shape, BF16),
            pltpu.VMEM((4 * width, nb * BS), BF16),
            pltpu.VMEM((4 * width, states), F32),
            pltpu.VMEM((nodes, *piece), BF16),
            pltpu.VMEM((nodes - 1, *piece), BF16),
            pltpu.VMEM((4, nodes // 4, *piece), BF16),
            pltpu.VMEM((3, nodes // 4, *piece), BF16),
            pltpu.VMEM((nodes // 4, *piece), BF16),
            pltpu.VMEM((nodes // 4 - 1, *piece), BF16),
            pltpu.SemaphoreType.DMA((6,)),
            pltpu.SemaphoreType.DMA((28,)),
            pltpu.SemaphoreType.DMA((28,)),
            pltpu.SemaphoreType.DMA,
            pltpu.SemaphoreType.DMA,
            pltpu.SemaphoreType.DMA((18,)),
            pltpu.SemaphoreType.DMA((18,)),
            pltpu.SemaphoreType.REGULAR((2,)),
        ],
        compiler_params=pltpu.CompilerParams(
            collective_id=0, has_side_effects=True, vmem_limit_bytes=55000 << 10
        ),
        name="project",
    )(panel.T, basis, g_blocks, c_blocks, block_cols.T)
    return reduced[0], reduced[1]


def solution(mesh):
    in_specs = (
        P("node", "col"),
        P("node", "col"),
        P("node", None, None, None),
        P("node", None, None, None),
        P("node", None),
    )
    out_specs = (P(("col", "node"), None), P(("col", "node"), None))
    return jax.shard_map(body, mesh=mesh, in_specs=in_specs, out_specs=out_specs, check_vma=False)
```

```python
import functools

import jax
import jax.numpy as jnp
from jax import lax
from jax.experimental import pallas as pl
from jax.experimental.pallas import tpu as pltpu
from jax.sharding import PartitionSpec as P

BS = 128
HB = 4
MESH = pl.DeviceIdType.MESH
F32, BF16 = jnp.float32, jnp.bfloat16
INNER = (4, 15, 26, 32, 34)
ROW_UNROLL = 15


def span(first, last):
    return pl.ds(first * BS, (last - first) * BS)


def kernel(
    nodes, xt, basis, gb, cb, bc_any, out,
    xl, xr, wi, we, wf, w0, w1, w2, w3, gv, cv, bv, yt, acc,
    stage, land, first, first_in, second, second_in, lsem, ssem, rsem, sum_send, sum_recv, part_send, part_recv, known, bc, bc_sem,
):
    nb = gb.shape[0]
    width = xt.shape[0]
    node, col = lax.axis_index("node"), lax.axis_index("col")
    core, x_lo = lax.rem(col, 2), col // 2
    y, z, x_hi = lax.rem(node, 4), lax.rem(node // 4, 8), node // 32
    above = (lax.rem(node + 1, nodes), col)
    below = (lax.rem(node + nodes - 1, nodes), col)
    above_beside = (above[0], col + 1 - 2 * core)
    below_beside = (below[0], col + 1 - 2 * core)
    across = (node, lax.rem(col + 2, 4))
    beside = (node, col + 1 - 2 * core)
    diagonal = (node, lax.rem(col + 2, 4) + 1 - 2 * core)
    mine = pl.ds(pl.multiple_of(core * width, width), width)

    loads = [pltpu.make_async_copy(xt, xl.at[mine, span(HB, HB + nb)], lsem.at[0])]
    half = nb // 2
    for k, (src, dst) in enumerate(((gb, gv), (cb, cv))):
        for part in range(2):
            rows = pl.ds(part * half, half)
            loads.append(pltpu.make_async_copy(src.at[rows], dst.at[rows], lsem.at[1 + 2 * part + k]))
    loads.append(pltpu.make_async_copy(basis, bv, lsem.at[5]))
    table = pltpu.make_async_copy(bc_any, bc, bc_sem)
    table.start()
    for load in (loads[0], loads[1], loads[3], loads[2], loads[4], loads[5]):
        load.start()

    barrier = pltpu.get_barrier_semaphore()
    y_line = [(node - y + lax.rem(y + d, 4), col) for d in (1, 2, 3)]
    z_line = [((x_hi * 8 + lax.rem(z + d, 8)) * 4 + y, col) for d in range(1, 8)]
    near = [across, beside, diagonal, (lax.rem(node + nodes // 2, nodes), col)] + y_line + z_line

    def greet(device):
        pl.semaphore_signal(barrier, inc=1, device_id=device, device_id_type=MESH)

    for peer in near:
        greet(peer)
    for peer in (above, below, above_beside, below_beside):
        greet(peer)
    pl.semaphore_wait(barrier, len(near) + 4)

    def tell(r):
        for peer in (y_line, z_line)[r]:
            pl.semaphore_signal(known.at[r], inc=1, device_id=peer, device_id_type=MESH)

    def hear(r):
        pl.semaphore_wait(known.at[r], len((y_line, z_line)[r]))

    made = []

    def remote(src, dst, device):
        k = len(made)
        made.append(
            pltpu.make_async_remote_copy(
                src_ref=src, dst_ref=dst, send_sem=ssem.at[k], recv_sem=rsem.at[k],
                device_id=device, device_id_type=MESH,
            )
        )
        return made[-1]

    chunks = [(0, HB), (nb - HB, nb)] + list(zip(INNER[:-1], INNER[1:]))
    lo, hi = span(0, HB), span(nb - HB, nb)
    halo_lo, halo_hi = span(0, HB), span(nb + HB, nb + 2 * HB)

    cross = [remote(xt.at[:, span(a, b)], xr.at[mine, span(a + HB, b + HB)], across) for a, b in chunks]
    pass_on = [
        remote(xr.at[mine, span(a + HB, b + HB)], xr.at[mine, span(a + HB, b + HB)], beside) for a, b in chunks[:-1]
    ]
    last = span(*chunks[-1])
    cross_both = remote(xt.at[:, last], xr.at[mine, span(INNER[-2] + HB, INNER[-1] + HB)], diagonal)
    own_up = [remote(xt.at[:, hi], xl.at[mine, halo_lo], to) for to in (above, above_beside)]
    own_down = [remote(xt.at[:, lo], xl.at[mine, halo_hi], to) for to in (below, below_beside)]
    own_body = remote(xt, xl.at[mine, span(HB, HB + nb)], beside)
    far_up = [remote(xr.at[mine, span(nb, nb + HB)], xr.at[mine, halo_lo], to) for to in (above, above_beside)]
    far_down = [remote(xr.at[mine, span(HB, 2 * HB)], xr.at[mine, halo_hi], to) for to in (below, below_beside)]

    for copy in (cross[0], cross[1], own_body, *own_up, *own_down, *cross[2:], cross_both):
        copy.start()

    def fill(window, slices, shift):
        for b in range(window.shape[0]):
            window[b] = slices[:, span(b + shift, b + shift + 1)]

    def products(window, first, last, shift):
        def tile(s, i):
            return window[jnp.clip(bc[s, i] - (node * nb - HB + shift), 0, window.shape[0] - 1)]

        def row(i):
            tiles = [tile(s, i) for s in range(3)]
            rhs = jnp.concatenate(
                [jnp.concatenate([m[i, s] for s in range(3)], axis=1) for m in (gv, cv)], axis=0
            )
            made_rows = lax.dot_general(
                jnp.concatenate(tiles, axis=1), rhs, (((1,), (1,)), ((), ())), preferred_element_type=F32
            ).astype(BF16)
            at = pl.ds(pl.multiple_of(i * BS, BS), BS)
            yt[: 2 * width, at] = made_rows[:, :BS]
            yt[2 * width :, at] = made_rows[:, BS:]

        count = last - first
        steps = count // ROW_UNROLL if count > ROW_UNROLL else 0

        def several(k, carry):
            for u in range(ROW_UNROLL):
                row(first + k * ROW_UNROLL + u)
            return carry

        if steps:
            lax.fori_loop(0, steps, several, 0)
        for i in range(first + steps * ROW_UNROLL, last):
            row(i)

    def project(first, last, fresh):
        rows = span(first, last)
        part = jnp.dot(yt[:, rows], bv[rows, :], preferred_element_type=F32)
        acc[...] = part if fresh else acc[...] + part

    to_x = [lax.rem(x_hi + d, 2) * 32 for d in (1, 0)]
    to_z = [lax.rem(z + d, 8) * 4 for d in (4, 3, 5, 2, 6, 1, 7, 0)]
    to_y = [lax.rem(y + d, 4) for d in (2, 1, 3, 0)]
    owners = [tx + tz + ty for tz in to_z for tx in to_x for ty in to_y][:-1]

    along_y = [
        pltpu.make_async_remote_copy(
            src_ref=first.at[to], dst_ref=first_in.at[k], send_sem=part_send.at[k], recv_sem=part_recv.at[k],
            device_id=(node - y + to, col), device_id_type=MESH,
        )
        for k, to in enumerate(to_y[:3])
    ]
    lines = [tx // 4 + tz // 4 for tz in to_z for tx in to_x]
    along_zx = [
        pltpu.make_async_remote_copy(
            src_ref=second.at[to], dst_ref=second_in.at[k], send_sem=part_send.at[3 + k], recv_sem=part_recv.at[3 + k],
            device_id=(to * 4 + y, col), device_id_type=MESH,
        )
        for k, to in enumerate(lines[:-1])
    ]

    def turned(s):
        return acc[:, s * BS : (s + 1) * BS].T.astype(BF16)

    def scatter_first():
        for s in range(acc.shape[1] // BS):
            tile = turned(s).reshape(4, 4, 8, acc.shape[0])
            for to in range(4):
                first[to, 4 * s : 4 * s + 4] = tile[:, to]
        for copy in along_y:
            copy.start()

    def pass_first():
        for copy in along_y:
            copy.wait_recv()
        for half_of in range(2):
            some = pl.ds(half_of * 8, 8)
            total = first[y, some].astype(F32)
            for k in range(3):
                total = total + first_in[k, some].astype(F32)
            second[some] = total.astype(BF16)
        for copy in along_zx:
            copy.start()

    def scatter_second():
        for s in range(acc.shape[1] // BS):
            stage[s * 16 : (s + 1) * 16] = turned(s).reshape(16, 8, acc.shape[0])
        for slot, to in enumerate(owners):
            pltpu.make_async_remote_copy(
                src_ref=stage.at[to], dst_ref=land.at[slot], send_sem=sum_send, recv_sem=sum_recv,
                device_id=(to, col), device_id_type=MESH,
            ).start()

    all_sums = pltpu.make_async_remote_copy(
        src_ref=stage.at[pl.ds(0, nodes - 1)], dst_ref=land, send_sem=sum_send, recv_sem=sum_recv,
        device_id=across, device_id_type=MESH,
    )

    def write(total, half_at):
        at = pl.ds(pl.multiple_of(half_at * 2 * width, 2 * width), 2 * width)
        out[0, :, at] = total[:, : 2 * width]
        out[1, :, at] = total[:, 2 * width :]

    def land_all(copies):
        for copy in copies:
            copy.wait_recv()

    tell(0)

    loads[0].wait()
    own_body.wait_recv()
    fill(wi, xl, HB)
    for load in loads[1:5]:
        load.wait()
    table.wait()
    products(wi, HB, nb // 2, HB)
    cross[0].wait_recv()
    pass_on[0].start()
    for copy in far_down:
        copy.start()
    cross[1].wait_recv()
    pass_on[1].start()
    for copy in far_up:
        copy.start()
    hear(0)
    tell(1)
    products(wi, nb // 2, nb - HB, HB)
    land_all(own_up)
    fill(we, xl, 0)
    products(we, 0, HB, 0)
    land_all(own_down)
    fill(wf, xl, nb - HB)
    products(wf, nb - HB, nb, nb - HB)
    cross[2].wait_recv()
    pass_on[2].start()
    loads[5].wait()
    project(0, nb, True)
    scatter_first()

    ends = [b - HB for b in INNER[1:-1]] + [nb]
    starts = [0] + ends[:-1]
    needs = (far_up + [pass_on[0], pass_on[2]], [pass_on[3]], [pass_on[4]], far_down + [pass_on[1], cross[5], cross_both])
    for p, (window, a, b) in enumerate(zip((w0, w1, w2, w3), starts, ends)):
        land_all(needs[p])
        fill(window, xr, a)
        products(window, a, b, a)
        project(a, b, p == 0)
        if p < 2:
            cross[3 + p].wait_recv()
            pass_on[3 + p].start()
        if p == 1:
            hear(1)
            pass_first()
    scatter_second()

    total = second[node // 4].astype(F32)
    for k, copy in enumerate(along_zx):
        copy.wait_recv()
        total = total + second_in[k].astype(F32)
    write(total, x_lo)
    all_sums.wait_recv()
    total = stage[node].astype(F32)
    for k in range(nodes - 1):
        total = total + land[k].astype(F32)
    write(total, 1 - x_lo)
    for copy in (*made, *along_y, *along_zx, all_sums):
        copy.wait_send()


def body(panel, basis, g_blocks, c_blocks, block_cols):
    nodes = lax.axis_size("node")
    nb = g_blocks.shape[0]
    width, states = panel.shape[1], basis.shape[1]
    ext = (nb + 2 * HB) * BS
    ends = [b - HB for b in INNER[1:-1]] + [nb]
    starts = [0] + ends[:-1]
    piece = (states // nodes, 4 * width)
    any_spec = pl.BlockSpec(memory_space=pl.ANY)
    vmem_spec = pl.BlockSpec(memory_space=pltpu.VMEM)
    windows = [(HB, nb - HB), (0, HB), (nb - HB, nb), *zip(starts, ends)]
    reduced = pl.pallas_call(
        functools.partial(kernel, nodes),
        out_shape=jax.ShapeDtypeStruct((2, *piece), F32),
        in_specs=[any_spec] * 5,
        out_specs=vmem_spec,
        scratch_shapes=[
            pltpu.VMEM((2 * width, ext), BF16),
            pltpu.VMEM((2 * width, ext), BF16),
            *[pltpu.VMEM((b - a + 2 * HB, 2 * width, BS), BF16) for a, b in windows],
            pltpu.VMEM(g_blocks.shape, BF16),
            pltpu.VMEM(c_blocks.shape, BF16),
            pltpu.VMEM(basis.shape, BF16),
            pltpu.VMEM((4 * width, nb * BS), BF16),
            pltpu.VMEM((4 * width, states), F32),
            pltpu.VMEM((nodes, *piece), BF16),
            pltpu.VMEM((nodes - 1, *piece), BF16),
            pltpu.VMEM((4, nodes // 4, *piece), BF16),
            pltpu.VMEM((3, nodes // 4, *piece), BF16),
            pltpu.VMEM((nodes // 4, *piece), BF16),
            pltpu.VMEM((nodes // 4 - 1, *piece), BF16),
            pltpu.SemaphoreType.DMA((6,)),
            pltpu.SemaphoreType.DMA((28,)),
            pltpu.SemaphoreType.DMA((28,)),
            pltpu.SemaphoreType.DMA,
            pltpu.SemaphoreType.DMA,
            pltpu.SemaphoreType.DMA((18,)),
            pltpu.SemaphoreType.DMA((18,)),
            pltpu.SemaphoreType.REGULAR((2,)),
            pltpu.SMEM(block_cols.shape[::-1], jnp.int32),
            pltpu.SemaphoreType.DMA,
        ],
        compiler_params=pltpu.CompilerParams(
            collective_id=0, has_side_effects=True, vmem_limit_bytes=55000 << 10
        ),
        name="project",
    )(panel.T, basis, g_blocks, c_blocks, block_cols.T)
    return reduced[0], reduced[1]


def solution(mesh):
    in_specs = (
        P("node", "col"),
        P("node", "col"),
        P("node", None, None, None),
        P("node", None, None, None),
        P("node", None),
    )
    out_specs = (P(("col", "node"), None), P(("col", "node"), None))
    return jax.shard_map(body, mesh=mesh, in_specs=in_specs, out_specs=out_specs, check_vma=False)
```

```python
import functools

import jax
import jax.numpy as jnp
from jax import lax
from jax.experimental import pallas as pl
from jax.experimental.pallas import tpu as pltpu
from jax.sharding import PartitionSpec as P

BS = 128
HB = 4
MESH = pl.DeviceIdType.MESH
F32, BF16 = jnp.float32, jnp.bfloat16
INNER = (4, 15, 26, 32, 34)
ROW_UNROLL = 15


def span(first, last):
    return pl.ds(first * BS, (last - first) * BS)


def kernel(
    nodes, xt, basis, gb, cb, bc_any, out,
    xl, xr, wi, we, wf, w0, w1, w2, w3, gv, cv, bv, yt, acc,
    stage, land, first, first_in, second, second_in, lsem, ssem, rsem, sum_send, sum_recv, part_send, part_recv, known, bc, bc_sem,
):
    nb = gb.shape[0]
    width = xt.shape[0]
    node, col = lax.axis_index("node"), lax.axis_index("col")
    core, x_lo = lax.rem(col, 2), col // 2
    y, z, x_hi = lax.rem(node, 4), lax.rem(node // 4, 8), node // 32
    above = (lax.rem(node + 1, nodes), col)
    below = (lax.rem(node + nodes - 1, nodes), col)
    above_beside = (above[0], col + 1 - 2 * core)
    below_beside = (below[0], col + 1 - 2 * core)
    across = (node, lax.rem(col + 2, 4))
    beside = (node, col + 1 - 2 * core)
    diagonal = (node, lax.rem(col + 2, 4) + 1 - 2 * core)
    mine = pl.ds(pl.multiple_of(core * width, width), width)

    loads = [pltpu.make_async_copy(xt, xl.at[mine, span(HB, HB + nb)], lsem.at[0])]
    half = nb // 2
    for k, (src, dst) in enumerate(((gb, gv), (cb, cv))):
        for part in range(2):
            rows = pl.ds(part * half, half)
            loads.append(pltpu.make_async_copy(src.at[rows], dst.at[rows], lsem.at[1 + 2 * part + k]))
    loads.append(pltpu.make_async_copy(basis, bv, lsem.at[5]))
    table = pltpu.make_async_copy(bc_any, bc, bc_sem)
    table.start()
    for load in (loads[0], loads[1], loads[3], loads[2], loads[4], loads[5]):
        load.start()

    barrier = pltpu.get_barrier_semaphore()
    y_line = [(node - y + lax.rem(y + d, 4), col) for d in (1, 2, 3)]
    z_line = [((x_hi * 8 + lax.rem(z + d, 8)) * 4 + y, col) for d in range(1, 8)]
    near = [across, beside, diagonal, (lax.rem(node + nodes // 2, nodes), col)] + y_line + z_line

    def greet(device):
        pl.semaphore_signal(barrier, inc=1, device_id=device, device_id_type=MESH)

    for peer in near:
        greet(peer)
    for peer in (above, below, above_beside, below_beside):
        greet(peer)
    pl.semaphore_wait(barrier, len(near) + 4)

    def tell(r):
        for peer in (y_line, z_line)[r]:
            pl.semaphore_signal(known.at[r], inc=1, device_id=peer, device_id_type=MESH)

    def hear(r):
        pl.semaphore_wait(known.at[r], len((y_line, z_line)[r]))

    made = []

    def remote(src, dst, device):
        k = len(made)
        made.append(
            pltpu.make_async_remote_copy(
                src_ref=src, dst_ref=dst, send_sem=ssem.at[k], recv_sem=rsem.at[k],
                device_id=device, device_id_type=MESH,
            )
        )
        return made[-1]

    chunks = [(0, HB), (nb - HB, nb)] + list(zip(INNER[:-1], INNER[1:]))
    lo, hi = span(0, HB), span(nb - HB, nb)
    halo_lo, halo_hi = span(0, HB), span(nb + HB, nb + 2 * HB)

    cross = [remote(xt.at[:, span(a, b)], xr.at[mine, span(a + HB, b + HB)], across) for a, b in chunks]
    pass_on = [
        remote(xr.at[mine, span(a + HB, b + HB)], xr.at[mine, span(a + HB, b + HB)], beside) for a, b in chunks[:-1]
    ]
    last = span(*chunks[-1])
    cross_both = remote(xt.at[:, last], xr.at[mine, span(INNER[-2] + HB, INNER[-1] + HB)], diagonal)
    own_up = [remote(xt.at[:, hi], xl.at[mine, halo_lo], to) for to in (above, above_beside)]
    own_down = [remote(xt.at[:, lo], xl.at[mine, halo_hi], to) for to in (below, below_beside)]
    own_body = remote(xt, xl.at[mine, span(HB, HB + nb)], beside)
    far_up = [remote(xr.at[mine, span(nb, nb + HB)], xr.at[mine, halo_lo], to) for to in (above, above_beside)]
    far_down = [remote(xr.at[mine, span(HB, 2 * HB)], xr.at[mine, halo_hi], to) for to in (below, below_beside)]

    for copy in (cross[0], cross[1], own_body, *own_up, *own_down, *cross[2:], cross_both):
        copy.start()

    def fill(window, slices, shift, blocks=None):
        for b in range(window.shape[0]) if blocks is None else blocks:
            window[b] = slices[:, span(b + shift, b + shift + 1)]

    def products(window, first, last, shift):
        def tile(s, i):
            return window[jnp.clip(bc[s, i] - (node * nb - HB + shift), 0, window.shape[0] - 1)]

        def row(i):
            tiles = [tile(s, i) for s in range(3)]
            rhs = jnp.concatenate(
                [jnp.concatenate([m[i, s] for s in range(3)], axis=1) for m in (gv, cv)], axis=0
            )
            made_rows = lax.dot_general(
                jnp.concatenate(tiles, axis=1), rhs, (((1,), (1,)), ((), ())), preferred_element_type=F32
            ).astype(BF16)
            at = pl.ds(pl.multiple_of(i * BS, BS), BS)
            yt[: 2 * width, at] = made_rows[:, :BS]
            yt[2 * width :, at] = made_rows[:, BS:]

        count = last - first
        steps = count // ROW_UNROLL if count > ROW_UNROLL else 0

        def several(k, carry):
            for u in range(ROW_UNROLL):
                row(first + k * ROW_UNROLL + u)
            return carry

        if steps:
            lax.fori_loop(0, steps, several, 0)
        for i in range(first + steps * ROW_UNROLL, last):
            row(i)

    def project(first, last, fresh):
        rows = span(first, last)
        part = jnp.dot(yt[:, rows], bv[rows, :], preferred_element_type=F32)
        acc[...] = part if fresh else acc[...] + part

    to_x = [lax.rem(x_hi + d, 2) * 32 for d in (1, 0)]
    to_z = [lax.rem(z + d, 8) * 4 for d in (4, 3, 5, 2, 6, 1, 7, 0)]
    to_y = [lax.rem(y + d, 4) for d in (2, 1, 3, 0)]
    owners = [tx + tz + ty for tz in to_z for tx in to_x for ty in to_y][:-1]

    along_y = [
        pltpu.make_async_remote_copy(
            src_ref=first.at[to], dst_ref=first_in.at[k], send_sem=part_send.at[k], recv_sem=part_recv.at[k],
            device_id=(node - y + to, col), device_id_type=MESH,
        )
        for k, to in enumerate(to_y[:3])
    ]
    lines = [tx // 4 + tz // 4 for tz in to_z for tx in to_x]
    along_zx = [
        pltpu.make_async_remote_copy(
            src_ref=second.at[to], dst_ref=second_in.at[k], send_sem=part_send.at[3 + k], recv_sem=part_recv.at[3 + k],
            device_id=(to * 4 + y, col), device_id_type=MESH,
        )
        for k, to in enumerate(lines[:-1])
    ]

    def turned(s):
        return acc[:, s * BS : (s + 1) * BS].T.astype(BF16)

    def scatter_first():
        for s in range(acc.shape[1] // BS):
            tile = turned(s).reshape(4, 4, 8, acc.shape[0])
            for to in range(4):
                first[to, 4 * s : 4 * s + 4] = tile[:, to]
        for copy in along_y:
            copy.start()

    def pass_first():
        for copy in along_y:
            copy.wait_recv()
        for half_of in range(2):
            some = pl.ds(half_of * 8, 8)
            total = first[y, some].astype(F32)
            for k in range(3):
                total = total + first_in[k, some].astype(F32)
            second[some] = total.astype(BF16)
        for copy in along_zx:
            copy.start()

    def scatter_second():
        for s in range(acc.shape[1] // BS):
            stage[s * 16 : (s + 1) * 16] = turned(s).reshape(16, 8, acc.shape[0])
        for slot, to in enumerate(owners):
            pltpu.make_async_remote_copy(
                src_ref=stage.at[to], dst_ref=land.at[slot], send_sem=sum_send, recv_sem=sum_recv,
                device_id=(to, col), device_id_type=MESH,
            ).start()

    all_sums = pltpu.make_async_remote_copy(
        src_ref=stage.at[pl.ds(0, nodes - 1)], dst_ref=land, send_sem=sum_send, recv_sem=sum_recv,
        device_id=across, device_id_type=MESH,
    )

    def write(total, half_at):
        at = pl.ds(pl.multiple_of(half_at * 2 * width, 2 * width), 2 * width)
        out[0, :, at] = total[:, : 2 * width]
        out[1, :, at] = total[:, 2 * width :]

    def land_all(copies):
        for copy in copies:
            copy.wait_recv()

    tell(0)

    loads[0].wait()
    own_body.wait_recv()
    fill(wi, xl, HB)
    for load in loads[1:5]:
        load.wait()
    table.wait()
    products(wi, HB, nb // 2, HB)
    cross[0].wait_recv()
    pass_on[0].start()
    for copy in far_down:
        copy.start()
    cross[1].wait_recv()
    pass_on[1].start()
    for copy in far_up:
        copy.start()
    hear(0)
    tell(1)
    products(wi, nb // 2, nb - HB, HB)
    land_all(own_up)
    fill(we, xl, 0)
    products(we, 0, HB, 0)
    land_all(own_down)
    fill(wf, xl, nb - HB)
    products(wf, nb - HB, nb, nb - HB)
    cross[2].wait_recv()
    pass_on[2].start()
    loads[5].wait()
    project(0, nb, True)
    scatter_first()

    ends = [b - HB for b in INNER[1:-1]] + [nb]
    starts = [0] + ends[:-1]
    needs = (far_up + [pass_on[0], pass_on[2]], [pass_on[3]], [pass_on[4]], far_down + [pass_on[1]])
    for p, (window, a, b) in enumerate(zip((w0, w1, w2, w3), starts, ends)):
        land_all(needs[p])
        late = [k - a for k in range(INNER[-2] + HB, INNER[-1] + HB)] if p == 3 else []
        fill(window, xr, a, [k for k in range(window.shape[0]) if k not in late])
        if late:
            land_all([cross[5], cross_both])
            fill(window, xr, a, late)
        products(window, a, b, a)
        project(a, b, p == 0)
        if p < 2:
            cross[3 + p].wait_recv()
            pass_on[3 + p].start()
        if p == 1:
            hear(1)
            pass_first()
    scatter_second()

    total = second[node // 4].astype(F32)
    for k, copy in enumerate(along_zx):
        copy.wait_recv()
        total = total + second_in[k].astype(F32)
    write(total, x_lo)
    all_sums.wait_recv()
    total = stage[node].astype(F32)
    for k in range(nodes - 1):
        total = total + land[k].astype(F32)
    write(total, 1 - x_lo)
    for copy in (*made, *along_y, *along_zx, all_sums):
        copy.wait_send()


def body(panel, basis, g_blocks, c_blocks, block_cols):
    nodes = lax.axis_size("node")
    nb = g_blocks.shape[0]
    width, states = panel.shape[1], basis.shape[1]
    ext = (nb + 2 * HB) * BS
    ends = [b - HB for b in INNER[1:-1]] + [nb]
    starts = [0] + ends[:-1]
    piece = (states // nodes, 4 * width)
    any_spec = pl.BlockSpec(memory_space=pl.ANY)
    vmem_spec = pl.BlockSpec(memory_space=pltpu.VMEM)
    windows = [(HB, nb - HB), (0, HB), (nb - HB, nb), *zip(starts, ends)]
    reduced = pl.pallas_call(
        functools.partial(kernel, nodes),
        out_shape=jax.ShapeDtypeStruct((2, *piece), F32),
        in_specs=[any_spec] * 5,
        out_specs=vmem_spec,
        scratch_shapes=[
            pltpu.VMEM((2 * width, ext), BF16),
            pltpu.VMEM((2 * width, ext), BF16),
            *[pltpu.VMEM((b - a + 2 * HB, 2 * width, BS), BF16) for a, b in windows],
            pltpu.VMEM(g_blocks.shape, BF16),
            pltpu.VMEM(c_blocks.shape, BF16),
            pltpu.VMEM(basis.shape, BF16),
            pltpu.VMEM((4 * width, nb * BS), BF16),
            pltpu.VMEM((4 * width, states), F32),
            pltpu.VMEM((nodes, *piece), BF16),
            pltpu.VMEM((nodes - 1, *piece), BF16),
            pltpu.VMEM((4, nodes // 4, *piece), BF16),
            pltpu.VMEM((3, nodes // 4, *piece), BF16),
            pltpu.VMEM((nodes // 4, *piece), BF16),
            pltpu.VMEM((nodes // 4 - 1, *piece), BF16),
            pltpu.SemaphoreType.DMA((6,)),
            pltpu.SemaphoreType.DMA((28,)),
            pltpu.SemaphoreType.DMA((28,)),
            pltpu.SemaphoreType.DMA,
            pltpu.SemaphoreType.DMA,
            pltpu.SemaphoreType.DMA((18,)),
            pltpu.SemaphoreType.DMA((18,)),
            pltpu.SemaphoreType.REGULAR((2,)),
            pltpu.SMEM(block_cols.shape[::-1], jnp.int32),
            pltpu.SemaphoreType.DMA,
        ],
        compiler_params=pltpu.CompilerParams(
            collective_id=0, has_side_effects=True, vmem_limit_bytes=55000 << 10
        ),
        name="project",
    )(panel.T, basis, g_blocks, c_blocks, block_cols.T)
    return reduced[0], reduced[1]


def solution(mesh):
    in_specs = (
        P("node", "col"),
        P("node", "col"),
        P("node", None, None, None),
        P("node", None, None, None),
        P("node", None),
    )
    out_specs = (P(("col", "node"), None), P(("col", "node"), None))
    return jax.shard_map(body, mesh=mesh, in_specs=in_specs, out_specs=out_specs, check_vma=False)
```
